32 devices in a mesh: section: 8 (over z, x), sp: 4 (over y, core).
Axes of the slice: x: 2, y: 2, z: 4, core: 2. Of those that a mesh axis runs over, the one named last changes fastest.
Arguments:
- slots: bfloat16 [8, 64, 3072], P('section', 'sp'), may hold values from -6 to 6
- patch_of_slot: int32 [8], replicated, may hold values from 0 to 7, each once
- step_of_slot: int32 [8], replicated, may hold values from 0 to 26
- modulation: bfloat16 [8, 28, 3, 3072], P('section'), may hold values from -4 to 4
- w_qkv: bfloat16 [8, 3072, 3, 2048], P('section', None, None, 'sp'), may hold values from -0.109375 to 0.109375
- qk_scale: bfloat16 [8, 2, 128], P('section'), may hold values from 0.25 to 4
- w_mlp_in: bfloat16 [8, 3072, 6144], P('section', None, 'sp'), may hold values from -0.109375 to 0.109375
- w_attn_out: bfloat16 [8, 2048, 3072], P('section', 'sp'), may hold values from -0.125 to 0.125
- w_mlp_out: bfloat16 [8, 6144, 3072], P('section', 'sp'), may hold values from -0.078125 to 0.078125
- kv_cache: bfloat16 [8, 2, 512, 2048], P('section', None, None, 'sp'), may hold values from -130 to 130
Outputs:
- slots_out: bfloat16 [8, 64, 3072], P('section', 'sp')
- kv_cache_out: bfloat16 [8, 2, 512, 2048], P('section', None, None, 'sp')
The draws below stay inside these ranges and needn't reach their ends.
Inputs may be any that keep to these rules, and one draw needn't show every extreme that they name: `patch_of_slot`: each patch id names exactly one slot.
All inputs are finite; a program needn't handle non-finite values.
Results may differ from the reference program's by a relative error of at most 0.012.
The reference program's roundings to bfloat16 on the way count: a program that leaves them out, or rounds other values in their place, can miss the bound.
Values may be sent and summed in bfloat16 or wider, within the bound.
A program may use at most 128 MiB of HBM per device.

```python
import math
import jax
import jax.numpy as jnp
from jax import lax

D = 3072
HD = 128
HEADS = 16
FF = 6144
STEPS = 28
ROUNDS = 2
LAYERS = 8
PATCHES = 8
PATCH_ROWS = 64
TOKENS = 512


def draw_qk_scale(key, part):
    key_b = jax.random.fold_in(jax.random.fold_in(key, 7), 1)
    array_shape = (LAYERS, 2, HD)
    exponent = jax.random.uniform(key_b, array_shape, jnp.float32, -1.3863, 1.3863)
    gains = jnp.exp(exponent)
    return gains.astype(jnp.bfloat16)


def draw_kv_cache(key, part):
    key_a, key_b = jax.random.split(key, 2)
    array_shape = (LAYERS, TOKENS, HEADS * HD)
    keys = jnp.clip(1.5 * jax.random.normal(key_a, array_shape, jnp.float32), -9.0, 9.0)
    values = jnp.clip(jax.random.normal(key_b, array_shape, jnp.float32), -6.0, 6.0)
    return jnp.stack([keys, values], axis=1).astype(jnp.bfloat16)


def plant(drawn, own_key, least, top_value):
    longest = drawn.shape.index(max(drawn.shape))
    spots = []
    for shift in (0, 1):
        where = [jax.random.randint(jax.random.fold_in(own_key, axis), (), 0, length) for axis, length in enumerate(drawn.shape)]
        where[longest] = (where[longest] + shift) % drawn.shape[longest]
        spots.append(tuple(where))
    return drawn.at[spots[0]].set(least).at[spots[1]].set(top_value)


def shard_levels(stream_key, extent, cuts, low, high):
    loudness, own = 1.0, jax.random.fold_in(stream_key, 6)
    for dim, blocks in cuts:
        draws = jnp.exp(jax.random.uniform(jax.random.fold_in(own, dim), (blocks,), jnp.float32, low / len(cuts), high / len(cuts)))
        loudness = loudness * jnp.repeat(draws, extent[dim] // blocks).reshape([-1 if axis == dim else 1 for axis in range(len(extent))])
    return loudness


def normal_values(key, extent, scale, reach, pieces=(), held_as=jnp.bfloat16):
    array = scale * jax.random.normal(key, extent, jnp.float32)
    if pieces:
        array = array * shard_levels(key, extent, pieces, -0.22, 0.18)
    return jnp.clip(array, -reach, reach).astype(held_as)


def setup_inputs(seed: int = 0) -> dict:
    streams_of = jax.random.split(jax.random.key(seed), 11)
    return {
        "slots": normal_values(streams_of[0], (PATCHES, PATCH_ROWS, D), 1.0, 6.0, ((0, 8), (1, 4))),
        "patch_of_slot": jax.random.permutation(streams_of[1], PATCHES).astype(jnp.int32),
        "step_of_slot": plant(jax.random.randint(streams_of[2], (PATCHES,), 0, STEPS - 1), jax.random.fold_in(streams_of[2], 1), 0, (STEPS - 1) - 1).astype(jnp.int32),
        "modulation": normal_values(streams_of[3], (LAYERS, STEPS, 3, D), 0.6, 4.0, ((0, 8),)),
        "w_qkv": normal_values(streams_of[4], (LAYERS, D, 3, HEADS * HD), D ** -0.5, 0.109375, ((0, 8), (3, 4))),
        "qk_scale": draw_qk_scale(jax.random.fold_in(streams_of[10], 71), 0),
        "w_mlp_in": normal_values(streams_of[6], (LAYERS, D, FF), D ** -0.5, 0.109375, ((0, 8), (2, 4))),
        "w_attn_out": normal_values(streams_of[7], (LAYERS, HEADS * HD, D), (HEADS * HD) ** -0.5, 0.125, ((0, 8), (1, 4))),
        "w_mlp_out": normal_values(streams_of[8], (LAYERS, FF, D), FF ** -0.5, 0.078125, ((0, 8), (1, 4))),
        "kv_cache": draw_kv_cache(jax.random.fold_in(streams_of[10], 71), 0),
    }


def head_norm(part, gain):
    rows = part.shape[0]
    wide = part.astype(jnp.float32).reshape(rows, -1, HD)
    power = lax.optimization_barrier(jnp.mean(wide * wide, axis=-1, keepdims=True))
    normed = wide * lax.rsqrt(power + 1e-06) * gain.astype(jnp.float32)
    return normed.astype(jnp.bfloat16).reshape(rows, -1)

def one_block(operands):
    slot, patch_id, timestep, table, qkv_weight, norm_gain, inner_weight, attention_weight, outer_weight, cache = operands
    factors = lax.dynamic_index_in_dim(table, timestep, 0, keepdims=False).astype(jnp.float32)
    wide = slot.astype(jnp.float32)
    center = wide - lax.optimization_barrier(jnp.mean(wide, axis=-1, keepdims=True))
    spread = lax.optimization_barrier(jnp.mean(center * center, axis=-1, keepdims=True))
    normed = (center * lax.rsqrt(spread + 1e-06) * (1.0 + factors[1]) + factors[0]).astype(jnp.bfloat16)
    projected = jnp.einsum('rd,dce->rce', normed.astype(jnp.float32), qkv_weight.astype(jnp.float32)).astype(jnp.bfloat16)
    query_normed = head_norm(projected[:, 0], norm_gain[0])
    key_normed = head_norm(projected[:, 1], norm_gain[1])
    first_row = (patch_id * PATCH_ROWS).astype(jnp.int32)
    keys = lax.dynamic_update_slice_in_dim(cache[0], key_normed, first_row, 0)
    values = lax.dynamic_update_slice_in_dim(cache[1], projected[:, 2], first_row, 0)
    queries = query_normed.astype(jnp.float32).reshape(PATCH_ROWS, HEADS, HD)
    key_heads = keys.astype(jnp.float32).reshape(TOKENS, HEADS, HD)
    value_heads = values.astype(jnp.float32).reshape(TOKENS, HEADS, HD)
    scores = jnp.einsum('rhd,thd->hrt', queries, key_heads) / math.sqrt(HD)
    shifted = jnp.exp(scores - lax.optimization_barrier(jnp.max(scores, axis=-1, keepdims=True)))
    weights = (shifted / lax.optimization_barrier(jnp.sum(shifted, axis=-1, keepdims=True))).astype(jnp.bfloat16)
    attention = jnp.einsum('hrt,thd->rhd', weights.astype(jnp.float32), value_heads).astype(jnp.bfloat16)
    attention = attention.reshape(PATCH_ROWS, HEADS * HD)
    activity = jax.nn.gelu(jnp.dot(normed, inner_weight, preferred_element_type=jnp.float32), approximate=True).astype(jnp.bfloat16)
    branch = jnp.dot(attention, attention_weight, preferred_element_type=jnp.float32) + jnp.dot(activity, outer_weight, preferred_element_type=jnp.float32)
    result = (wide + factors[2] * branch).astype(jnp.bfloat16)
    return (result, jnp.stack([keys, values]))

def reference(slots, patch_of_slot, step_of_slot, modulation, w_qkv, qk_scale, w_mlp_in, w_attn_out, w_mlp_out, kv_cache):
    current = slots
    cache = kv_cache
    patch_ids = patch_of_slot
    timesteps = step_of_slot
    first_slot = (jnp.arange(PATCHES) == 0).astype(jnp.int32)
    for round_id in range(ROUNDS):
        current, cache = lax.map(one_block, (current, patch_ids, timesteps, modulation, w_qkv, qk_scale, w_mlp_in, w_attn_out, w_mlp_out, cache))
        current = jnp.roll(current, 1, axis=0)
        patch_ids = jnp.roll(patch_ids, 1)
        timesteps = jnp.roll(timesteps, 1) + first_slot
    return (current, cache)
```

```python
import functools
import math

import jax
import jax.numpy as jnp
from jax import lax
from jax.experimental import pallas as pl
from jax.experimental.pallas import tpu as pltpu
from jax.sharding import PartitionSpec as P

HD = 128
ROUNDS = 2
F32 = jnp.float32
BF16 = jnp.bfloat16
MESH = pl.DeviceIdType.MESH


def divides(total, wanted):
    return max(size for size in range(128, wanted + 1, 128) if total % size == 0)


def kernel(sections, peers, patch_ref, step_ref, slots_ref, mod_ref, gain_ref,
           qkv_hbm, inner_hbm, attn_hbm, outer_hbm, kv_hbm,
           x_out, kv_out,
           qkv, inner, attn_w, outer, kv, gathered, landed, part, whole, fresh, arrived,
           h_buf, a_buf, act_buf, factors, load_sem, kv_sem, out_sem,
           ag_send, ag_recv, rs_send, rs_recv, sh_send, sh_recv):
    rows, width = slots_ref.shape
    total_rows = peers * rows
    heads = qkv.shape[2] // HD
    hidden = inner.shape[1]
    tokens = kv.shape[1]
    chunks = rs_send.shape[1]
    cut = width // chunks
    in_cut = divides(hidden, 512)
    in_chunks = hidden // in_cut
    me = lax.axis_index("sp")
    sid = lax.axis_index("section")
    following = lax.rem(sid + 1, sections)
    previous = lax.rem(sid + sections - 1, sections)

    loads = []

    def load(source, target):
        copy = pltpu.make_async_copy(source, target, load_sem.at[len(loads)])
        loads.append(copy)
        return copy

    qkv_loads = [load(qkv_hbm.at[i], qkv.at[i]) for i in range(3)]
    inner_loads = [
        load(inner_hbm.at[:, pl.ds(i * in_cut, in_cut)], inner.at[:, pl.ds(i * in_cut, in_cut)])
        for i in range(in_chunks)
    ]
    out_loads = []
    for c in range(chunks):
        span = pl.ds(c * cut, cut)
        out_loads.append(
            (load(attn_hbm.at[:, span], attn_w.at[:, span]),
             load(outer_hbm.at[:, span], outer.at[:, span]))
        )
    kv_load = pltpu.make_async_copy(kv_hbm, kv, kv_sem)
    for copy in qkv_loads:
        copy.start()
    kv_load.start()
    for copy in loads[3:]:
        copy.start()

    barrier = pltpu.get_barrier_semaphore()
    for k in range(1, peers):
        pl.semaphore_signal(barrier, inc=1, device_id={"sp": lax.rem(me + k, peers)}, device_id_type=MESH)
    for other in (following, previous):
        pl.semaphore_signal(barrier, inc=1, device_id={"section": other}, device_id_type=MESH)
    pl.semaphore_wait(barrier, peers - 1 + 2)

    sends = []
    gathers = [[], []]
    for k in range(1, peers):
        copy = pltpu.make_async_remote_copy(
            src_ref=slots_ref, dst_ref=gathered.at[0, me],
            send_sem=ag_send.at[0, 0, k], recv_sem=ag_recv.at[0, 0, k],
            device_id={"sp": lax.rem(me + k, peers)}, device_id_type=MESH)
        copy.start()
        gathers[0].append(copy)
        sends.append(copy)
    gathered[0, me] = slots_ref[...]

    for r in range(ROUNDS):
        anchor = sid - r
        wrapped = (anchor < 0).astype(jnp.int32)
        anchor = anchor + wrapped * sections
        patch = patch_ref[anchor]
        step = step_ref[anchor] + wrapped
        table_rows = lax.broadcasted_iota(jnp.int32, (mod_ref.shape[1], width), 0)
        for i in range(3):
            picked = jnp.where(table_rows == step, mod_ref[i].astype(F32), 0.0)
            factors[i : i + 1, :] = jnp.sum(picked, axis=0, keepdims=True)
        shift = factors[0:1, :]
        scale = 1.0 + factors[1:2, :]

        if r > 0:
            for c in range(chunks):
                span = pl.ds(c * cut, cut)
                shifts[c].wait_recv()
                for k in range(1, peers):
                    copy = pltpu.make_async_remote_copy(
                        src_ref=gathered.at[r, me, :, span], dst_ref=gathered.at[r, me, :, span],
                        send_sem=ag_send.at[r, c, k], recv_sem=ag_recv.at[r, c, k],
                        device_id={"sp": lax.rem(me + k, peers)}, device_id_type=MESH)
                    copy.start()
                    gathers[r].append(copy)
                    sends.append(copy)
        for copy in gathers[r]:
            copy.wait_recv()
        for n in range(peers):
            wide = gathered[r, n].astype(F32)
            center = wide - jnp.mean(wide, axis=-1, keepdims=True)
            spread = jnp.mean(center * center, axis=-1, keepdims=True)
            h_buf[n * rows : (n + 1) * rows, :] = (
                center * lax.rsqrt(spread + 1e-06) * scale + shift
            ).astype(BF16)

        made = []
        for i in range(3):
            if r == 0:
                qkv_loads[i].wait()
            made.append(jnp.dot(h_buf[...], qkv[i], preferred_element_type=F32).astype(BF16))
        if r == 0:
            kv_load.wait()

        def head_norm(value, head, which):
            one = value[:, head * HD : (head + 1) * HD].astype(F32)
            power = jnp.mean(one * one, axis=-1, keepdims=True)
            return (one * lax.rsqrt(power + 1e-06) * gain_ref[which : which + 1, :].astype(F32)).astype(BF16)

        for head in range(heads):
            lanes = slice(head * HD, (head + 1) * HD)
            query = head_norm(made[0], head, 0)
            key = head_norm(made[1], head, 1)
            value = made[2][:, lanes]
            for p in range(tokens // total_rows):
                there = slice(p * total_rows, (p + 1) * total_rows)
                hit = jnp.broadcast_to(patch, (total_rows, HD)) == p
                kv[0, there, lanes] = jnp.where(hit, key.astype(F32), kv[0, there, lanes].astype(F32)).astype(BF16)
                kv[1, there, lanes] = jnp.where(hit, value.astype(F32), kv[1, there, lanes].astype(F32)).astype(BF16)
            scores = lax.dot_general(
                query, kv[0, :, lanes], (((1,), (1,)), ((), ())), preferred_element_type=F32
            ) / math.sqrt(HD)
            raised = jnp.exp(scores - jnp.max(scores, axis=-1, keepdims=True))
            probs = (raised / jnp.sum(raised, axis=-1, keepdims=True)).astype(BF16)
            a_buf[:, lanes] = jnp.dot(probs, kv[1, :, lanes], preferred_element_type=F32).astype(BF16)
        if r == ROUNDS - 1:
            kv_store = pltpu.make_async_copy(kv, kv_out, out_sem)
            kv_store.start()

        for i in range(in_chunks):
            if r == 0:
                inner_loads[i].wait()
            span = slice(i * in_cut, (i + 1) * in_cut)
            act_buf[:, span] = jax.nn.gelu(
                jnp.dot(h_buf[...], inner[:, span], preferred_element_type=F32), approximate=True
            ).astype(BF16)

        reduces = []
        for c in range(chunks):
            if r == 0:
                out_loads[c][0].wait()
                out_loads[c][1].wait()
            lanes = slice(c * cut, (c + 1) * cut)
            span = pl.ds(c * cut, cut)
            share = jnp.dot(a_buf[...], attn_w[:, lanes], preferred_element_type=F32)
            share = share + jnp.dot(act_buf[...], outer[:, lanes], preferred_element_type=F32)
            for n in range(peers):
                block = share[n * rows : (n + 1) * rows, :]
                whole[n, :, lanes] = block
                part[r, n, :, lanes] = block.astype(BF16)
            group = []
            for k in range(1, peers):
                to = lax.rem(me + k, peers)
                copy = pltpu.make_async_remote_copy(
                    src_ref=part.at[r, to, :, span], dst_ref=landed.at[r, k, :, span],
                    send_sem=rs_send.at[r, c, k], recv_sem=rs_recv.at[r, c, k],
                    device_id={"sp": to}, device_id_type=MESH)
                copy.start()
                group.append(copy)
                sends.append(copy)
            reduces.append(group)

        shifts = []
        for c in range(chunks):
            lanes = slice(c * cut, (c + 1) * cut)
            span = pl.ds(c * cut, cut)
            for copy in reduces[c]:
                copy.wait_recv()
            summed = whole[me, :, lanes]
            for k in range(1, peers):
                summed = summed + landed[r, k, :, lanes].astype(F32)
            fresh[r, :, lanes] = (
                gathered[r, me, :, lanes].astype(F32) + factors[2:3, lanes] * summed
            ).astype(BF16)
            target = gathered.at[r + 1, me, :, span] if r < ROUNDS - 1 else arrived.at[:, span]
            copy = pltpu.make_async_remote_copy(
                src_ref=fresh.at[r, :, span], dst_ref=target,
                send_sem=sh_send.at[r, c], recv_sem=sh_recv.at[r, c],
                device_id={"section": following}, device_id_type=MESH)
            copy.start()
            shifts.append(copy)
            sends.append(copy)

    for copy in shifts:
        copy.wait_recv()
    x_out[...] = arrived[...]
    kv_store.wait()
    for copy in sends:
        copy.wait_send()


def shards(sections, peers, slots, patch_of_slot, step_of_slot, modulation, w_qkv, qk_scale,
           w_mlp_in, w_attn_out, w_mlp_out, kv_cache):
    rows, width = slots.shape[1:]
    local = w_qkv.shape[3]
    hidden = w_mlp_in.shape[2]
    total_rows = peers * rows
    tokens = kv_cache.shape[2]
    chunks = width // divides(width, 768)
    loads = 3 + hidden // divides(hidden, 512) + 2 * chunks
    dma = pltpu.SemaphoreType.DMA
    vmem = pl.BlockSpec(memory_space=pltpu.VMEM)
    smem = pl.BlockSpec(memory_space=pltpu.SMEM)
    anywhere = pl.BlockSpec(memory_space=pl.ANY)
    x, kv = pl.pallas_call(
        functools.partial(kernel, sections, peers),
        out_shape=(
            jax.ShapeDtypeStruct((rows, width), BF16),
            jax.ShapeDtypeStruct(kv_cache.shape[1:], BF16),
        ),
        in_specs=[smem, smem, vmem, vmem, vmem] + [anywhere] * 5,
        out_specs=(vmem, anywhere),
        scratch_shapes=[
            pltpu.VMEM((3, width, local), BF16),
            pltpu.VMEM((width, hidden), BF16),
            pltpu.VMEM((local, width), BF16),
            pltpu.VMEM((hidden, width), BF16),
            pltpu.VMEM((2, tokens, local), BF16),
            pltpu.VMEM((ROUNDS, peers, rows, width), BF16),
            pltpu.VMEM((ROUNDS, peers, rows, width), BF16),
            pltpu.VMEM((ROUNDS, peers, rows, width), BF16),
            pltpu.VMEM((peers, rows, width), F32),
            pltpu.VMEM((ROUNDS, rows, width), BF16),
            pltpu.VMEM((rows, width), BF16),
            pltpu.VMEM((total_rows, width), BF16),
            pltpu.VMEM((total_rows, local), BF16),
            pltpu.VMEM((total_rows, hidden), BF16),
            pltpu.VMEM((8, width), F32),
            dma((loads,)),
            dma,
            dma,
            dma((ROUNDS, chunks, peers)),
            dma((ROUNDS, chunks, peers)),
            dma((ROUNDS, chunks, peers)),
            dma((ROUNDS, chunks, peers)),
            dma((ROUNDS, chunks)),
            dma((ROUNDS, chunks)),
        ],
        compiler_params=pltpu.CompilerParams(
            collective_id=0, has_side_effects=True, vmem_limit_bytes=60 * 1024 * 1024
        ),
    )(
        patch_of_slot, step_of_slot, slots[0], jnp.transpose(modulation[0], (1, 0, 2)), qk_scale[0],
        jnp.transpose(w_qkv[0], (1, 0, 2)), w_mlp_in[0], w_attn_out[0], w_mlp_out[0], kv_cache[0],
    )
    return (x[None], kv[None])


def solution(mesh):
    return jax.shard_map(
        functools.partial(shards, mesh.shape["section"], mesh.shape["sp"]),
        mesh=mesh,
        in_specs=(
            P("section", "sp", None),
            P(),
            P(),
            P("section", None, None, None),
            P("section", None, None, "sp"),
            P("section", None, None),
            P("section", None, "sp"),
            P("section", "sp", None),
            P("section", "sp", None),
            P("section", None, None, "sp"),
        ),
        out_specs=(P("section", "sp", None), P("section", None, None, "sp")),
        check_vma=False,
    )
```

```python
import functools
import math

import jax
import jax.numpy as jnp
from jax import lax
from jax.experimental import pallas as pl
from jax.experimental.pallas import tpu as pltpu
from jax.sharding import PartitionSpec as P

HD = 128
ROUNDS = 2
F32 = jnp.float32
BF16 = jnp.bfloat16
MESH = pl.DeviceIdType.MESH


def divides(total, wanted):
    return max(size for size in range(128, wanted + 1, 128) if total % size == 0)


def kernel(sections, peers, patch_ref, step_ref, slots_ref, mod_ref, gain_ref,
           qkv_hbm, inner_hbm, attn_hbm, outer_hbm, kv_hbm,
           x_out, kv_out,
           qkv, inner, attn_w, outer, kv, gathered, landed, paired, part, mid, whole, fresh, arrived,
           h_buf, a_buf, act_buf, factors, load_sem, kv_sem, out_sem,
           ag_send, ag_recv, rs_send, rs_recv, sh_send, sh_recv):
    rows, width = slots_ref.shape
    total_rows = peers * rows
    heads = qkv.shape[2] // HD
    hidden = inner.shape[1]
    tokens = kv.shape[1]
    chunks = rs_send.shape[1]
    cut = width // chunks
    in_cut = divides(hidden, 512)
    in_chunks = hidden // in_cut
    me = lax.axis_index("sp")
    groups = peers // 2
    group = me // 2
    core = lax.rem(me, 2)
    partner = group * 2 + 1 - core

    def alike(k):
        return lax.rem(group + k, groups)

    def spread_rows(r, c, source):
        span = pl.ds(c * cut, cut)
        across, beside = [], []
        for k in range(1, groups):
            across.append(remote(
                source, gathered.at[r, me, :, span], ag_send.at[r, c, k], ag_recv.at[r, c, k],
                {"sp": alike(k) * 2 + core}))
        beside.append(remote(
            source, gathered.at[r, me, :, span], ag_send.at[r, c, groups], ag_recv.at[r, c, groups],
            {"sp": partner}))
        return across, beside

    def relay_rows(r, c, across, beside):
        span = pl.ds(c * cut, cut)
        for k in range(1, groups):
            across[k - 1].wait_recv()
            block = gathered.at[r, alike(groups - k) * 2 + core, :, span]
            beside.append(remote(
                block, block, ag_send.at[r, c, groups + k], ag_recv.at[r, c, groups + k],
                {"sp": partner}))

    sends = []

    def remote(source, target, send_sem, recv_sem, device):
        copy = pltpu.make_async_remote_copy(
            src_ref=source, dst_ref=target, send_sem=send_sem, recv_sem=recv_sem,
            device_id=device, device_id_type=MESH)
        copy.start()
        sends.append(copy)
        return copy

    sid = lax.axis_index("section")
    following = lax.rem(sid + 1, sections)
    previous = lax.rem(sid + sections - 1, sections)

    loads = []

    def load(source, target):
        copy = pltpu.make_async_copy(source, target, load_sem.at[len(loads)])
        loads.append(copy)
        return copy

    qkv_loads = [load(qkv_hbm.at[i], qkv.at[i]) for i in range(3)]
    inner_loads = [
        load(inner_hbm.at[:, pl.ds(i * in_cut, in_cut)], inner.at[:, pl.ds(i * in_cut, in_cut)])
        for i in range(in_chunks)
    ]
    out_loads = []
    for c in range(chunks):
        span = pl.ds(c * cut, cut)
        out_loads.append(
            (load(attn_hbm.at[:, span], attn_w.at[:, span]),
             load(outer_hbm.at[:, span], outer.at[:, span]))
        )
    kv_load = pltpu.make_async_copy(kv_hbm, kv, kv_sem)
    for copy in qkv_loads:
        copy.start()
    kv_load.start()
    for copy in loads[3:]:
        copy.start()

    barrier = pltpu.get_barrier_semaphore()
    for k in range(1, peers):
        pl.semaphore_signal(barrier, inc=1, device_id={"sp": lax.rem(me + k, peers)}, device_id_type=MESH)
    for other in (following, previous):
        pl.semaphore_signal(barrier, inc=1, device_id={"section": other}, device_id_type=MESH)
    pl.semaphore_wait(barrier, peers - 1 + 2)

    moves = [spread_rows(0, c, slots_ref.at[:, pl.ds(c * cut, cut)]) for c in range(chunks)]
    gathered[0, me] = slots_ref[...]

    for r in range(ROUNDS):
        anchor = sid - r
        wrapped = (anchor < 0).astype(jnp.int32)
        anchor = anchor + wrapped * sections
        patch = patch_ref[anchor]
        step = step_ref[anchor] + wrapped
        table_rows = lax.broadcasted_iota(jnp.int32, (mod_ref.shape[1], width), 0)
        for i in range(3):
            picked = jnp.where(table_rows == step, mod_ref[i].astype(F32), 0.0)
            factors[i : i + 1, :] = jnp.sum(picked, axis=0, keepdims=True)
        shift = factors[0:1, :]
        scale = 1.0 + factors[1:2, :]

        if r > 0:
            moves = []
            for c in range(chunks):
                shifts[c].wait_recv()
                moves.append(spread_rows(r, c, gathered.at[r, me, :, pl.ds(c * cut, cut)]))
                if c > 0:
                    relay_rows(r, c - 1, *moves[c - 1])
            relay_rows(r, chunks - 1, *moves[chunks - 1])
        else:
            for c in range(chunks):
                relay_rows(r, c, *moves[c])
        for _, beside in moves:
            for copy in beside:
                copy.wait_recv()
        for n in range(peers):
            wide = gathered[r, n].astype(F32)
            center = wide - jnp.mean(wide, axis=-1, keepdims=True)
            spread = jnp.mean(center * center, axis=-1, keepdims=True)
            h_buf[n * rows : (n + 1) * rows, :] = (
                center * lax.rsqrt(spread + 1e-06) * scale + shift
            ).astype(BF16)

        made = []
        for i in range(3):
            if r == 0:
                qkv_loads[i].wait()
            made.append(jnp.dot(h_buf[...], qkv[i], preferred_element_type=F32).astype(BF16))
        if r == 0:
            kv_load.wait()

        def head_norm(value, head, which):
            one = value[:, head * HD : (head + 1) * HD].astype(F32)
            power = jnp.mean(one * one, axis=-1, keepdims=True)
            return (one * lax.rsqrt(power + 1e-06) * gain_ref[which : which + 1, :].astype(F32)).astype(BF16)

        for head in range(heads):
            lanes = slice(head * HD, (head + 1) * HD)
            query = head_norm(made[0], head, 0)
            key = head_norm(made[1], head, 1)
            value = made[2][:, lanes]
            for p in range(tokens // total_rows):
                there = slice(p * total_rows, (p + 1) * total_rows)
                hit = jnp.broadcast_to(patch, (total_rows, HD)) == p
                kv[0, there, lanes] = jnp.where(hit, key.astype(F32), kv[0, there, lanes].astype(F32)).astype(BF16)
                kv[1, there, lanes] = jnp.where(hit, value.astype(F32), kv[1, there, lanes].astype(F32)).astype(BF16)
            scores = lax.dot_general(
                query, kv[0, :, lanes], (((1,), (1,)), ((), ())), preferred_element_type=F32
            ) / math.sqrt(HD)
            raised = jnp.exp(scores - jnp.max(scores, axis=-1, keepdims=True))
            probs = (raised / jnp.sum(raised, axis=-1, keepdims=True)).astype(BF16)
            a_buf[:, lanes] = jnp.dot(probs, kv[1, :, lanes], preferred_element_type=F32).astype(BF16)
        if r == ROUNDS - 1:
            kv_store = pltpu.make_async_copy(kv, kv_out, out_sem)
            kv_store.start()

        for i in range(in_chunks):
            if r == 0:
                inner_loads[i].wait()
            span = slice(i * in_cut, (i + 1) * in_cut)
            act_buf[:, span] = jax.nn.gelu(
                jnp.dot(h_buf[...], inner[:, span], preferred_element_type=F32), approximate=True
            ).astype(BF16)

        pairs, reduces = [], []

        def pass_on(c):
            lanes = slice(c * cut, (c + 1) * cut)
            span = pl.ds(c * cut, cut)
            pairs[c].wait_recv()
            crossing = []
            for k in range(1, groups):
                to = alike(k)
                mid[r, k, :, lanes] = (
                    whole[to * 2 + core, :, lanes] + paired[r, to, :, lanes].astype(F32)
                ).astype(BF16)
                crossing.append(remote(
                    mid.at[r, k, :, span], landed.at[r, k, :, span],
                    rs_send.at[r, c, k], rs_recv.at[r, c, k], {"sp": to * 2 + core}))
            reduces.append(crossing)

        for c in range(chunks):
            if r == 0:
                out_loads[c][0].wait()
                out_loads[c][1].wait()
            lanes = slice(c * cut, (c + 1) * cut)
            span = pl.ds(c * cut, cut)
            share = jnp.dot(a_buf[...], attn_w[:, lanes], preferred_element_type=F32)
            share = share + jnp.dot(act_buf[...], outer[:, lanes], preferred_element_type=F32)
            for n in range(peers):
                block = share[n * rows : (n + 1) * rows, :]
                whole[n, :, lanes] = block
                part[r, n % 2, n // 2, :, lanes] = block.astype(BF16)
            pairs.append(remote(
                part.at[r, 1 - core, :, :, span], paired.at[r, :, :, span],
                rs_send.at[r, c, 0], rs_recv.at[r, c, 0], {"sp": partner}))
            if c > 0:
                pass_on(c - 1)
        pass_on(chunks - 1)

        shifts = []
        for c in range(chunks):
            lanes = slice(c * cut, (c + 1) * cut)
            span = pl.ds(c * cut, cut)
            for copy in reduces[c]:
                copy.wait_recv()
            summed = whole[me, :, lanes] + paired[r, group, :, lanes].astype(F32)
            for k in range(1, groups):
                summed = summed + landed[r, k, :, lanes].astype(F32)
            fresh[r, :, lanes] = (
                gathered[r, me, :, lanes].astype(F32) + factors[2:3, lanes] * summed
            ).astype(BF16)
            target = gathered.at[r + 1, me, :, span] if r < ROUNDS - 1 else arrived.at[:, span]
            shifts.append(remote(
                fresh.at[r, :, span], target, sh_send.at[r, c], sh_recv.at[r, c], {"section": following}))

    for copy in shifts:
        copy.wait_recv()
    x_out[...] = arrived[...]
    kv_store.wait()
    for copy in sends:
        copy.wait_send()


def shards(sections, peers, slots, patch_of_slot, step_of_slot, modulation, w_qkv, qk_scale,
           w_mlp_in, w_attn_out, w_mlp_out, kv_cache):
    rows, width = slots.shape[1:]
    local = w_qkv.shape[3]
    hidden = w_mlp_in.shape[2]
    total_rows = peers * rows
    tokens = kv_cache.shape[2]
    chunks = width // divides(width, 768)
    loads = 3 + hidden // divides(hidden, 512) + 2 * chunks
    dma = pltpu.SemaphoreType.DMA
    vmem = pl.BlockSpec(memory_space=pltpu.VMEM)
    smem = pl.BlockSpec(memory_space=pltpu.SMEM)
    anywhere = pl.BlockSpec(memory_space=pl.ANY)
    x, kv = pl.pallas_call(
        functools.partial(kernel, sections, peers),
        out_shape=(
            pltpu.VMEM((rows, width), BF16),
            pltpu.VMEM(kv_cache.shape[1:], BF16),
        ),
        in_specs=[smem, smem, vmem, vmem, vmem] + [anywhere] * 5,
        out_specs=(vmem, vmem),
        scratch_shapes=[
            pltpu.VMEM((3, width, local), BF16),
            pltpu.VMEM((width, hidden), BF16),
            pltpu.VMEM((local, width), BF16),
            pltpu.VMEM((hidden, width), BF16),
            pltpu.VMEM((2, tokens, local), BF16),
            pltpu.VMEM((ROUNDS, peers, rows, width), BF16),
            pltpu.VMEM((ROUNDS, peers // 2, rows, width), BF16),
            pltpu.VMEM((ROUNDS, peers // 2, rows, width), BF16),
            pltpu.VMEM((ROUNDS, 2, peers // 2, rows, width), BF16),
            pltpu.VMEM((ROUNDS, peers // 2, rows, width), BF16),
            pltpu.VMEM((peers, rows, width), F32),
            pltpu.VMEM((ROUNDS, rows, width), BF16),
            pltpu.VMEM((rows, width), BF16),
            pltpu.VMEM((total_rows, width), BF16),
            pltpu.VMEM((total_rows, local), BF16),
            pltpu.VMEM((total_rows, hidden), BF16),
            pltpu.VMEM((8, width), F32),
            dma((loads,)),
            dma,
            dma,
            dma((ROUNDS, chunks, peers)),
            dma((ROUNDS, chunks, peers)),
            dma((ROUNDS, chunks, peers)),
            dma((ROUNDS, chunks, peers)),
            dma((ROUNDS, chunks)),
            dma((ROUNDS, chunks)),
        ],
        compiler_params=pltpu.CompilerParams(
            collective_id=0, has_side_effects=True, vmem_limit_bytes=60 * 1024 * 1024
        ),
    )(
        patch_of_slot, step_of_slot, slots[0], jnp.transpose(modulation[0], (1, 0, 2)), qk_scale[0],
        jnp.transpose(w_qkv[0], (1, 0, 2)), w_mlp_in[0], w_attn_out[0], w_mlp_out[0], kv_cache[0],
    )
    return (x[None], kv[None])


def solution(mesh):
    return jax.shard_map(
        functools.partial(shards, mesh.shape["section"], mesh.shape["sp"]),
        mesh=mesh,
        in_specs=(
            P("section", "sp", None),
            P(),
            P(),
            P("section", None, None, None),
            P("section", None, None, "sp"),
            P("section", None, None),
            P("section", None, "sp"),
            P("section", "sp", None),
            P("section", "sp", None),
            P("section", None, None, "sp"),
        ),
        out_specs=(P("section", "sp", None), P("section", None, None, "sp")),
        check_vma=False,
    )
```

```python
import functools
import math

import jax
import jax.numpy as jnp
from jax import lax
from jax.experimental import pallas as pl
from jax.experimental.pallas import tpu as pltpu
from jax.sharding import PartitionSpec as P

HD = 128
ROUNDS = 2
F32 = jnp.float32
BF16 = jnp.bfloat16
MESH = pl.DeviceIdType.MESH


def divides(total, wanted):
    return max(size for size in range(128, wanted + 1, 128) if total % size == 0)


def kernel(sections, peers, patch_ref, step_ref, slots_ref, mod_ref, gain_ref,
           qkv_hbm, inner_hbm, attn_hbm, outer_hbm, kv_hbm,
           x_out, kv_out,
           qkv, inner, attn_w, outer, kv, gathered, landed, part, whole, fresh, arrived,
           h_buf, a_buf, act_buf, factors, load_sem, kv_sem, out_sem,
           ag_send, ag_recv, rs_send, rs_recv, sh_send, sh_recv):
    rows, width = slots_ref.shape
    total_rows = peers * rows
    heads = qkv.shape[2] // HD
    hidden = inner.shape[1]
    tokens = kv.shape[1]
    chunks = rs_send.shape[1]
    cut = width // chunks
    in_cut = divides(hidden, 512)
    in_chunks = hidden // in_cut
    me = lax.axis_index("sp")
    sid = lax.axis_index("section")
    following = lax.rem(sid + 1, sections)
    previous = lax.rem(sid + sections - 1, sections)

    loads = []

    def load(source, target):
        copy = pltpu.make_async_copy(source, target, load_sem.at[len(loads)])
        loads.append(copy)
        return copy

    qkv_loads = [load(qkv_hbm.at[i], qkv.at[i]) for i in range(3)]
    inner_loads = [
        load(inner_hbm.at[:, pl.ds(i * in_cut, in_cut)], inner.at[:, pl.ds(i * in_cut, in_cut)])
        for i in range(in_chunks)
    ]
    out_loads = []
    for c in range(chunks):
        span = pl.ds(c * cut, cut)
        out_loads.append(
            (load(attn_hbm.at[:, span], attn_w.at[:, span]),
             load(outer_hbm.at[:, span], outer.at[:, span]))
        )
    kv_load = pltpu.make_async_copy(kv_hbm, kv, kv_sem)
    for copy in qkv_loads:
        copy.start()

    barrier = pltpu.get_barrier_semaphore()
    for k in range(1, peers):
        pl.semaphore_signal(barrier, inc=1, device_id={"sp": lax.rem(me + k, peers)}, device_id_type=MESH)
    for other in (following, previous):
        pl.semaphore_signal(barrier, inc=1, device_id={"section": other}, device_id_type=MESH)
    pl.semaphore_wait(barrier, peers - 1 + 2)

    sends = []
    gathers = [[], []]
    for k in range(1, peers):
        copy = pltpu.make_async_remote_copy(
            src_ref=slots_ref, dst_ref=gathered.at[0, me],
            send_sem=ag_send.at[0, 0, k], recv_sem=ag_recv.at[0, 0, k],
            device_id={"sp": lax.rem(me + k, peers)}, device_id_type=MESH)
        copy.start()
        gathers[0].append(copy)
        sends.append(copy)
    kv_load.start()
    for copy in loads[3:]:
        copy.start()
    gathered[0, me] = slots_ref[...]

    for r in range(ROUNDS):
        anchor = sid - r
        wrapped = (anchor < 0).astype(jnp.int32)
        anchor = anchor + wrapped * sections
        patch = patch_ref[anchor]
        step = step_ref[anchor] + wrapped
        table_rows = lax.broadcasted_iota(jnp.int32, (mod_ref.shape[1], width), 0)
        for i in range(3):
            picked = jnp.where(table_rows == step, mod_ref[i].astype(F32), 0.0)
            factors[i : i + 1, :] = jnp.sum(picked, axis=0, keepdims=True)
        shift = factors[0:1, :]
        scale = 1.0 + factors[1:2, :]

        if r > 0:
            for c in range(chunks):
                span = pl.ds(c * cut, cut)
                shifts[c].wait_recv()
                for k in range(1, peers):
                    copy = pltpu.make_async_remote_copy(
                        src_ref=gathered.at[r, me, :, span], dst_ref=gathered.at[r, me, :, span],
                        send_sem=ag_send.at[r, c, k], recv_sem=ag_recv.at[r, c, k],
                        device_id={"sp": lax.rem(me + k, peers)}, device_id_type=MESH)
                    copy.start()
                    gathers[r].append(copy)
                    sends.append(copy)
        for copy in gathers[r]:
            copy.wait_recv()
        for n in range(peers):
            wide = gathered[r, n].astype(F32)
            center = wide - jnp.mean(wide, axis=-1, keepdims=True)
            spread = jnp.mean(center * center, axis=-1, keepdims=True)
            h_buf[n * rows : (n + 1) * rows, :] = (
                center * lax.rsqrt(spread + 1e-06) * scale + shift
            ).astype(BF16)

        made = []
        for i in range(3):
            if r == 0:
                qkv_loads[i].wait()
            made.append(jnp.dot(h_buf[...], qkv[i], preferred_element_type=F32).astype(BF16))
        if r == 0:
            kv_load.wait()

        def head_norm(value, head, which):
            one = value[:, head * HD : (head + 1) * HD].astype(F32)
            power = jnp.mean(one * one, axis=-1, keepdims=True)
            return (one * lax.rsqrt(power + 1e-06) * gain_ref[which : which + 1, :].astype(F32)).astype(BF16)

        for head in range(heads):
            lanes = slice(head * HD, (head + 1) * HD)
            query = head_norm(made[0], head, 0)
            key = head_norm(made[1], head, 1)
            value = made[2][:, lanes]
            for p in range(tokens // total_rows):
                there = slice(p * total_rows, (p + 1) * total_rows)
                hit = jnp.broadcast_to(patch, (total_rows, HD)) == p
                kv[0, there, lanes] = jnp.where(hit, key.astype(F32), kv[0, there, lanes].astype(F32)).astype(BF16)
                kv[1, there, lanes] = jnp.where(hit, value.astype(F32), kv[1, there, lanes].astype(F32)).astype(BF16)
            scores = lax.dot_general(
                query, kv[0, :, lanes], (((1,), (1,)), ((), ())), preferred_element_type=F32
            ) / math.sqrt(HD)
            raised = jnp.exp(scores - jnp.max(scores, axis=-1, keepdims=True))
            probs = (raised / jnp.sum(raised, axis=-1, keepdims=True)).astype(BF16)
            a_buf[:, lanes] = jnp.dot(probs, kv[1, :, lanes], preferred_element_type=F32).astype(BF16)
        if r == ROUNDS - 1:
            kv_store = pltpu.make_async_copy(kv, kv_out, out_sem)
            kv_store.start()

        for i in range(in_chunks):
            if r == 0:
                inner_loads[i].wait()
            span = slice(i * in_cut, (i + 1) * in_cut)
            act_buf[:, span] = jax.nn.gelu(
                jnp.dot(h_buf[...], inner[:, span], preferred_element_type=F32), approximate=True
            ).astype(BF16)

        reduces = []
        for c in range(chunks):
            if r == 0:
                out_loads[c][0].wait()
                out_loads[c][1].wait()
            lanes = slice(c * cut, (c + 1) * cut)
            span = pl.ds(c * cut, cut)
            share = jnp.dot(a_buf[...], attn_w[:, lanes], preferred_element_type=F32)
            share = share + jnp.dot(act_buf[...], outer[:, lanes], preferred_element_type=F32)
            for n in range(peers):
                block = share[n * rows : (n + 1) * rows, :]
                whole[n, :, lanes] = block
                part[r, n, :, lanes] = block.astype(BF16)
            group = []
            for k in range(1, peers):
                to = lax.rem(me + k, peers)
                copy = pltpu.make_async_remote_copy(
                    src_ref=part.at[r, to, :, span], dst_ref=landed.at[r, k, :, span],
                    send_sem=rs_send.at[r, c, k], recv_sem=rs_recv.at[r, c, k],
                    device_id={"sp": to}, device_id_type=MESH)
                copy.start()
                group.append(copy)
                sends.append(copy)
            reduces.append(group)

        shifts = []
        for c in range(chunks):
            lanes = slice(c * cut, (c + 1) * cut)
            span = pl.ds(c * cut, cut)
            for copy in reduces[c]:
                copy.wait_recv()
            summed = whole[me, :, lanes]
            for k in range(1, peers):
                summed = summed + landed[r, k, :, lanes].astype(F32)
            fresh[r, :, lanes] = (
                gathered[r, me, :, lanes].astype(F32) + factors[2:3, lanes] * summed
            ).astype(BF16)
            target = gathered.at[r + 1, me, :, span] if r < ROUNDS - 1 else arrived.at[:, span]
            copy = pltpu.make_async_remote_copy(
                src_ref=fresh.at[r, :, span], dst_ref=target,
                send_sem=sh_send.at[r, c], recv_sem=sh_recv.at[r, c],
                device_id={"section": following}, device_id_type=MESH)
            copy.start()
            shifts.append(copy)
            sends.append(copy)

    for copy in shifts:
        copy.wait_recv()
    x_out[...] = arrived[...]
    kv_store.wait()
    for copy in sends:
        copy.wait_send()


def shards(sections, peers, slots, patch_of_slot, step_of_slot, modulation, w_qkv, qk_scale,
           w_mlp_in, w_attn_out, w_mlp_out, kv_cache):
    rows, width = slots.shape[1:]
    local = w_qkv.shape[3]
    hidden = w_mlp_in.shape[2]
    total_rows = peers * rows
    tokens = kv_cache.shape[2]
    chunks = width // divides(width, 768)
    loads = 3 + hidden // divides(hidden, 512) + 2 * chunks
    dma = pltpu.SemaphoreType.DMA
    vmem = pl.BlockSpec(memory_space=pltpu.VMEM)
    smem = pl.BlockSpec(memory_space=pltpu.SMEM)
    anywhere = pl.BlockSpec(memory_space=pl.ANY)
    x, kv = pl.pallas_call(
        functools.partial(kernel, sections, peers),
        out_shape=(
            pltpu.VMEM((rows, width), BF16),
            pltpu.VMEM(kv_cache.shape[1:], BF16),
        ),
        in_specs=[smem, smem, vmem, vmem, vmem] + [anywhere] * 5,
        out_specs=(vmem, vmem),
        scratch_shapes=[
            pltpu.VMEM((3, width, local), BF16),
            pltpu.VMEM((width, hidden), BF16),
            pltpu.VMEM((local, width), BF16),
            pltpu.VMEM((hidden, width), BF16),
            pltpu.VMEM((2, tokens, local), BF16),
            pltpu.VMEM((ROUNDS, peers, rows, width), BF16),
            pltpu.VMEM((ROUNDS, peers, rows, width), BF16),
            pltpu.VMEM((ROUNDS, peers, rows, width), BF16),
            pltpu.VMEM((peers, rows, width), F32),
            pltpu.VMEM((ROUNDS, rows, width), BF16),
            pltpu.VMEM((rows, width), BF16),
            pltpu.VMEM((total_rows, width), BF16),
            pltpu.VMEM((total_rows, local), BF16),
            pltpu.VMEM((total_rows, hidden), BF16),
            pltpu.VMEM((8, width), F32),
            dma((loads,)),
            dma,
            dma,
            dma((ROUNDS, chunks, peers)),
            dma((ROUNDS, chunks, peers)),
            dma((ROUNDS, chunks, peers)),
            dma((ROUNDS, chunks, peers)),
            dma((ROUNDS, chunks)),
            dma((ROUNDS, chunks)),
        ],
        compiler_params=pltpu.CompilerParams(
            collective_id=0, has_side_effects=True, vmem_limit_bytes=60 * 1024 * 1024
        ),
    )(
        patch_of_slot, step_of_slot, slots[0], jnp.transpose(modulation[0], (1, 0, 2)), qk_scale[0],
        jnp.transpose(w_qkv[0], (1, 0, 2)), w_mlp_in[0], w_attn_out[0], w_mlp_out[0], kv_cache[0],
    )
    return (x[None], kv[None])


def solution(mesh):
    return jax.shard_map(
        functools.partial(shards, mesh.shape["section"], mesh.shape["sp"]),
        mesh=mesh,
        in_specs=(
            P("section", "sp", None),
            P(),
            P(),
            P("section", None, None, None),
            P("section", None, None, "sp"),
            P("section", None, None),
            P("section", None, "sp"),
            P("section", "sp", None),
            P("section", "sp", None),
            P("section", None, None, "sp"),
        ),
        out_specs=(P("section", "sp", None), P("section", None, None, "sp")),
        check_vma=False,
    )
```
